32 devices in a mesh: dp: 2 (over x), seq: 8 (over z, core), tensor: 2 (over y).
Axes of the slice: x: 2, y: 2, z: 4, core: 2. Of those that a mesh axis runs over, the one named last changes fastest.
Arguments:
- events: bfloat16 [4, 2048, 1536], P('dp', 'seq', 'tensor'), may hold values from -6 to 6
- gate_in: bfloat16 [4, 2048, 1536], P('dp', 'seq', 'tensor'), may hold values from -6 to 6
- filters: bfloat16 [1024, 1536], P(None, 'tensor'), may hold values from -0.1875 to 0.1875
- proj: bfloat16 [1536, 1536], P('tensor'), may hold values from -0.15625 to 0.15625
- lengths: int32 [4], P('dp'), may hold values from 256 to 2048, as said below
- cotangent: bfloat16 [4, 2048, 1536], P('dp', 'seq', 'tensor'), may hold values from -6 to 6
Outputs:
- mixed: bfloat16 [4, 2048, 1536], P('dp', 'seq', 'tensor')
- grad_input: bfloat16 [4, 2048, 1536], P('dp', 'seq', 'tensor')
- grad_gate: bfloat16 [4, 2048, 1536], P('dp', 'seq', 'tensor')
- grad_filters: float32 [1024, 1536], P(None, 'tensor')
- grad_proj: float32 [1536, 1536], P('tensor')
The draws below stay inside these ranges and needn't reach their ends.
Inputs may be any that keep to these rules, and one draw needn't show every extreme that they name: `lengths`: each length is a multiple of 256, and some user's length is 2048.
All inputs are finite; a program needn't handle non-finite values.
Results may differ from the reference program's by a relative error of at most 0.0049.
Values may be sent and summed in bfloat16 or wider, within the bound.
No kernel may reach another device: no remote copies, remote signals or barrier semaphores. Data moves between devices by JAX's collectives and lax.ppermute only.
A program may use at most 128 MiB of HBM per device.

```python
import math
import jax
import jax.numpy as jnp
from jax import lax

D = 1536
TAPS = 1024
BLK = 256
SEQLEN = 2048
USERS = 4


def draw_lengths(key, part):
    blocks = jax.random.randint(key, (USERS,), 1, SEQLEN // BLK + 1)
    blocks = blocks.at[0].set(SEQLEN // BLK)
    return (blocks * BLK).astype(jnp.int32)


def steps_of(stream_key, shape, cuts, low, top_value):
    level, own = 1.0, jax.random.fold_in(stream_key, 6)
    for dim, parts in cuts:
        draws = jnp.exp(jax.random.uniform(jax.random.fold_in(own, dim), (parts,), jnp.float32, low / len(cuts), top_value / len(cuts)))
        level = level * jnp.repeat(draws, shape[dim] // parts).reshape([-1 if axis == dim else 1 for axis in range(len(shape))])
    return level


def gaussian(rng, shape, spread, reach, shards=(), kind=jnp.bfloat16):
    level = steps_of(rng, shape, shards, -0.22, 0.18) if shards else 1.0
    drawn = jax.random.normal(rng, shape, jnp.float32) * spread * level
    return jnp.minimum(jnp.maximum(drawn, -reach), reach).astype(kind)


def setup_inputs(seed: int = 0) -> dict:
    arg_keys = jax.random.split(jax.random.key(seed), 7)
    return {
        "events": gaussian(arg_keys[0], (USERS, SEQLEN, D), 1.0, 6.0, ((0, 2), (1, 8), (2, 2))),
        "gate_in": gaussian(arg_keys[1], (USERS, SEQLEN, D), 1.5, 6.0, ((0, 2), (1, 8), (2, 2))),
        "filters": gaussian(arg_keys[2], (TAPS, D), TAPS ** -0.5, 0.1875, ((1, 2),)),
        "proj": gaussian(arg_keys[3], (D, D), D ** -0.5, 0.15625, ((0, 2),)),
        "lengths": draw_lengths(jax.random.fold_in(arg_keys[6], 71), 0),
        "cotangent": gaussian(arg_keys[5], (USERS, SEQLEN, D), 1.0, 6.0, ((0, 2), (1, 8), (2, 2))),
    }


def fft_length():
    return 2 ** int(math.ceil(math.log2(SEQLEN + TAPS)))

def reference(events, gate_in, filters, proj, lengths, cotangent):
    nfft = fft_length()
    position = jnp.arange(SEQLEN, dtype=jnp.int32)
    live = (position[None, :] < lengths[:, None]).astype(jnp.float32)[:, :, None]
    masked = (events.astype(jnp.float32) * live).astype(jnp.bfloat16)
    filter_spec = jnp.fft.rfft(filters.astype(jnp.float32), nfft, axis=0)

    def causal_one(rows):
        spec = jnp.fft.rfft(rows.astype(jnp.float32), nfft, axis=0)
        return jnp.fft.irfft(spec * filter_spec, nfft, axis=0)[:SEQLEN].astype(jnp.float32)
    conv = lax.map(causal_one, masked)
    gate_f = gate_in.astype(jnp.float32)
    gate_sig = jax.nn.sigmoid(gate_f)
    silu_g = gate_f * gate_sig
    gated = (silu_g * conv * live).astype(jnp.bfloat16)
    gated_rows = gated.reshape(-1, D)
    mixed = jnp.dot(gated_rows, proj, preferred_element_type=jnp.float32).astype(jnp.bfloat16).reshape(USERS, SEQLEN, D)
    cot_rows = cotangent.reshape(-1, D)
    grad_gated = jnp.dot(cot_rows, proj.T, preferred_element_type=jnp.float32).reshape(USERS, SEQLEN, D) * live
    grad_conv = (grad_gated * silu_g).astype(jnp.bfloat16)
    grad_gate = (grad_gated * conv * gate_sig * (1.0 + gate_f * (1.0 - gate_sig))).astype(jnp.bfloat16)

    def ahead_one(rows):
        spec = jnp.fft.rfft(rows.astype(jnp.float32), nfft, axis=0)
        return jnp.fft.irfft(spec * jnp.conj(filter_spec), nfft, axis=0)[:SEQLEN].astype(jnp.float32)
    grad_input = (lax.map(ahead_one, grad_conv) * live).astype(jnp.bfloat16)

    def lag_one(pair):
        source, grads = pair
        spec_m = jnp.fft.rfft(source.astype(jnp.float32), nfft, axis=0)
        spec_g = jnp.fft.rfft(grads.astype(jnp.float32), nfft, axis=0)
        return jnp.fft.irfft(spec_g * jnp.conj(spec_m), nfft, axis=0)[:TAPS].astype(jnp.float32)
    scale = 1.0 / math.sqrt(USERS * SEQLEN)
    grad_filters = lax.optimization_barrier(jnp.sum(lax.map(lag_one, (masked, grad_conv)), axis=0)) * scale
    grad_proj = jnp.dot(gated_rows.T, cot_rows, preferred_element_type=jnp.float32) * scale
    return (mixed, grad_input, grad_gate, grad_filters, grad_proj)
```

```python
import functools
import math

import jax
import jax.numpy as jnp
import numpy as np
from jax import lax
from jax.experimental import pallas as pl
from jax.experimental.pallas import tpu as pltpu
from jax.sharding import PartitionSpec as P

F32 = jnp.float32
BF16 = jnp.bfloat16


def tables(block):
    size = 2 * block
    freq = np.concatenate([np.arange(0, block, 2), np.arange(1, block, 2)])
    turn = ((2 * freq[:, None] + 1) * np.arange(block)[None, :]) % (2 * size)
    angle = turn * (np.pi / size)
    full = np.concatenate([np.cos(angle), np.sin(angle)], axis=0)
    inv = full.T / block

    def pair(table):
        high = table.astype(jnp.bfloat16)
        low = (table - high.astype(np.float64)).astype(jnp.bfloat16)
        return high, low

    fwd = np.concatenate(pair(full), axis=1)
    inv_high, inv_low = pair(inv)
    return fwd, np.concatenate([inv_high, inv_high, inv_low], axis=1)


def forward(tab_ref, block):
    twice = jnp.concatenate([block, block], axis=0)
    return jnp.dot(tab_ref[...], twice, preferred_element_type=F32)


def backward(inv_ref, z_ref, at, size):
    both = jnp.dot(inv_ref[:, : 2 * size], z_ref[at], preferred_element_type=F32)
    rest = jnp.dot(inv_ref[:, 2 * size :], z_ref[at, :size], preferred_element_type=F32)
    return both + rest


def put_split(z_ref, at, rows, size, lanes, value):
    high = value.astype(BF16)
    z_ref[at, rows, lanes] = high
    low = pl.ds(rows.start + size, rows.size)
    z_ref[at, low, lanes] = (value - high.astype(F32)).astype(BF16)


def lane_parts(chans):
    return [slice(lo, min(lo + 128, chans)) for lo in range(0, chans, 128)]


def filter_kernel(taps_ref, tab_ref, out_ref, spec):
    size, block = tab_ref.shape[0], tab_ref.shape[0] // 2
    reach = taps_ref.shape[0] // block
    half = block // 2
    for j in range(reach):
        spec[j] = forward(tab_ref, taps_ref[j * block : (j + 1) * block])
    for e in range(reach + 1):
        for odd in range(2):
            sign = -1.0 if odd else 1.0
            cs = slice(odd * half, (odd + 1) * half)
            sn = slice(block + odd * half, block + (odd + 1) * half)
            if e == 0:
                real, imag = spec[0, cs], spec[0, sn]
            elif e == reach:
                real, imag = sign * spec[e - 1, sn], -sign * spec[e - 1, cs]
            else:
                real = spec[e, cs] + sign * spec[e - 1, sn]
                imag = spec[e, sn] - sign * spec[e - 1, cs]
            out_ref[e, cs] = real
            out_ref[e, sn] = imag


def pick_block(refs, choice, parity, user):
    if isinstance(choice, int):
        return refs[choice][user]
    even, odd = choice
    return jnp.where(parity == 0, refs[even][user], refs[odd][user])


def conv_kernel(choices, n_blocks, scal_ref, *refs):
    blocks = refs[:n_blocks]
    (grad_ref, gate_ref, gg_ref, e_ref, tab_ref, inv_ref) = refs[n_blocks : n_blocks + 6]
    gated_ref, ggate_ref, fg_ref = refs[n_blocks + 6 : n_blocks + 9]
    spec, gspec, z_ref = refs[n_blocks + 9 :]
    users, block, chans = grad_ref.shape
    size = 2 * block
    reach = len(choices) - 1
    half = block // 2
    parity = scal_ref[0]
    row = lax.broadcasted_iota(jnp.int32, (block, chans), 0)
    for u in range(users):
        gspec[u] = forward(tab_ref, grad_ref[u])
        for e in range(reach + 1):
            count = scal_ref[1 + e * users + u]
            value = pick_block(blocks, choices[e], parity, u)
            value = jnp.where(row < count, value.astype(F32), 0.0).astype(BF16)
            spec[e, u] = forward(tab_ref, value)

    step = 16
    for odd in range(2):
        sign = -1.0 if odd else 1.0

        @pl.loop(0, half // step)
        def _(t):
            base = pl.multiple_of(odd * half + t * step, step)
            cs, sn = pl.ds(base, step), pl.ds(block + base, step)
            for lanes in lane_parts(chans):
                g = [(gspec[u, cs, lanes], gspec[u, sn, lanes]) for u in range(users)]
                y = [None] * users
                before = None
                for e in range(reach + 1):
                    ec, es = e_ref[e, cs, lanes], e_ref[e, sn, lanes]
                    wc = ws = None
                    for u in range(users):
                        ac, as_ = spec[e, u, cs, lanes], spec[e, u, sn, lanes]
                        gc, gs = g[u]
                        yc, ys = ac * ec - as_ * es, ac * es + as_ * ec
                        y[u] = (yc, ys) if e == 0 else (y[u][0] + yc, y[u][1] + ys)
                        pc, ps = gc * ac + gs * as_, gs * ac - gc * as_
                        wc, ws = (pc, ps) if u == 0 else (wc + pc, ws + ps)
                    if before is not None:
                        at = users + e - 1
                        put_split(z_ref, at, cs, size, lanes, before[0] - sign * ws)
                        put_split(z_ref, at, sn, size, lanes, before[1] + sign * wc)
                    before = (wc, ws)
                for u in range(users):
                    put_split(z_ref, u, cs, size, lanes, y[u][0])
                    put_split(z_ref, u, sn, size, lanes, y[u][1])

    for u in range(users):
        conv = backward(inv_ref, z_ref, u, size)
        gate = gate_ref[u].astype(F32)
        sig = jax.nn.sigmoid(gate)
        live = (row < scal_ref[1 + u]).astype(F32)
        gated_ref[u] = (gate * sig * conv * live).astype(BF16)
        ggate_ref[u] = (gg_ref[u] * conv * sig * (1.0 + gate * (1.0 - sig))).astype(BF16)
    for j in range(reach):
        fg_ref[j] = backward(inv_ref, z_ref, users + j, size)


def input_kernel(choices, n_blocks, scal_ref, *refs):
    blocks = refs[:n_blocks]
    e_ref, tab_ref, inv_ref, out_ref, spec, z_ref = refs[n_blocks:]
    users, block, chans = blocks[0].shape
    size = 2 * block
    reach = len(choices) - 1
    parity = scal_ref[0]
    row = lax.broadcasted_iota(jnp.int32, (block, chans), 0)
    for u in range(users):
        for e in range(reach + 1):
            spec[e, u] = forward(tab_ref, pick_block(blocks, choices[e], parity, u))

    step = 16

    @pl.loop(0, block // step)
    def _(t):
        base = pl.multiple_of(t * step, step)
        cs, sn = pl.ds(base, step), pl.ds(block + base, step)
        for lanes in lane_parts(chans):
            z = [None] * users
            for e in range(reach + 1):
                ec, es = e_ref[e, cs, lanes], e_ref[e, sn, lanes]
                for u in range(users):
                    gc, gs = spec[e, u, cs, lanes], spec[e, u, sn, lanes]
                    zc, zs = gc * ec + gs * es, gs * ec - gc * es
                    z[u] = (zc, zs) if e == 0 else (z[u][0] + zc, z[u][1] + zs)
            for u in range(users):
                put_split(z_ref, u, cs, size, lanes, z[u][0])
                put_split(z_ref, u, sn, size, lanes, z[u][1])

    for u in range(users):
        value = backward(inv_ref, z_ref, u, size)
        out_ref[u] = jnp.where(row < scal_ref[1 + u], value, 0.0).astype(BF16)


def chan_tile(chans):
    return 256 if chans % 256 == 0 else chans


def whole(array):
    return pl.BlockSpec(array.shape, lambda c, *_: (0,) * array.ndim)


def by_chans(shape, tile):
    return pl.BlockSpec(
        shape[:-1] + (tile,), lambda c, *_: (0,) * (len(shape) - 1) + (c,)
    )


def cost(flops, size):
    return pl.CostEstimate(flops=flops, bytes_accessed=size, transcendentals=0)


def filter_spectra(filters, fwd):
    taps_len, chans = filters.shape
    size = fwd.shape[0]
    reach = taps_len // (size // 2)
    tile = chan_tile(chans)
    out = jax.ShapeDtypeStruct((reach + 1, size, chans), F32)
    return pl.pallas_call(
        filter_kernel,
        grid=(chans // tile,),
        in_specs=[by_chans(filters.shape, tile), whole(fwd)],
        out_specs=by_chans(out.shape, tile),
        out_shape=out,
        scratch_shapes=[pltpu.VMEM((reach, size, tile), F32)],
        cost_estimate=cost(2 * reach * size * size * chans, out.size * 4),
        name="filter_spectra",
    )(filters, fwd)


def conv_call(scal, choices, blocks, grad_conv, gate, grad_gated, spectra, fwd, inv):
    users, block, chans = grad_conv.shape
    size = 2 * block
    reach = len(choices) - 1
    tile = chan_tile(chans)
    outs = [
        jax.ShapeDtypeStruct(gate.shape, BF16),
        jax.ShapeDtypeStruct(gate.shape, BF16),
        jax.ShapeDtypeStruct((reach, block, chans), F32),
    ]
    moved = [*blocks, grad_conv, gate, grad_gated, spectra]
    grid_spec = pltpu.PrefetchScalarGridSpec(
        num_scalar_prefetch=1,
        grid=(chans // tile,),
        in_specs=[by_chans(a.shape, tile) for a in moved] + [whole(fwd), whole(inv)],
        out_specs=[by_chans(o.shape, tile) for o in outs],
        scratch_shapes=[
            pltpu.VMEM((reach + 1, users, size, tile), F32),
            pltpu.VMEM((users, size, tile), F32),
            pltpu.VMEM((users + reach, 2 * size, tile), BF16),
        ],
    )
    flops = 2 * chans * size * size * ((reach + 2) * users + 2 * (users + reach))
    return pl.pallas_call(
        functools.partial(conv_kernel, choices, len(blocks)),
        grid_spec=grid_spec,
        out_shape=outs,
        cost_estimate=cost(flops, sum(a.size * a.dtype.itemsize for a in moved)),
        name="conv",
    )(scal, *moved, fwd, inv)


def input_call(scal, choices, blocks, spectra, fwd, inv):
    users, block, chans = blocks[0].shape
    size = 2 * block
    reach = len(choices) - 1
    tile = chan_tile(chans)
    moved = [*blocks, spectra]
    out = jax.ShapeDtypeStruct(blocks[0].shape, BF16)
    grid_spec = pltpu.PrefetchScalarGridSpec(
        num_scalar_prefetch=1,
        grid=(chans // tile,),
        in_specs=[by_chans(a.shape, tile) for a in moved] + [whole(fwd), whole(inv)],
        out_specs=by_chans(out.shape, tile),
        scratch_shapes=[
            pltpu.VMEM((reach + 1, users, size, tile), F32),
            pltpu.VMEM((users, 2 * size, tile), BF16),
        ],
    )
    flops = 2 * chans * size * size * ((reach + 1) * users + 2 * users)
    return pl.pallas_call(
        functools.partial(input_kernel, choices, len(blocks)),
        grid_spec=grid_spec,
        out_shape=out,
        cost_estimate=cost(flops, sum(a.size * a.dtype.itemsize for a in moved)),
        name="grad_input",
    )(scal, *moved, fwd, inv)


def shifted(value, axis, by):
    count = lax.axis_size(axis)
    pairs = [(i, i + by) for i in range(count) if 0 <= i + by < count]
    return lax.ppermute(value, axis, pairs)


def swapped(value, axis, bit, only=None):
    pairs = [(i, i ^ bit) for i in range(lax.axis_size(axis))]
    if only is not None:
        pairs = [(i, j) for i, j in pairs if i % 2 == only]
    return lax.ppermute(value, axis, pairs)


def halo(value, reach, way):
    count = lax.axis_size("seq")
    if reach != 4 or count % 2:
        arrays = [value] + [shifted(value, "seq", way * k) for k in range(1, reach + 1)]
        return arrays, list(range(reach + 1))
    one = shifted(value, "seq", 2 * way)
    near = 0 if way == 1 else 1
    own_swap = swapped(value, "seq", 1, only=near)
    two = shifted(one, "seq", 2 * way)
    one_swap = swapped(one, "seq", 1)
    two_swap = swapped(two, "seq", 1, only=1 - near)
    arrays = [value, own_swap, one, one_swap, two, two_swap]
    if way == 1:
        return arrays, [0, (3, 1), 2, (5, 3), 4]
    return arrays, [0, (1, 3), 2, (3, 5), 4]


def is_power(n):
    return n & (n - 1) == 0


def sum_stages():
    dp, seq = lax.axis_size("dp"), lax.axis_size("seq")
    if not (is_power(dp) and is_power(seq)):
        return None
    stages = [("seq", 1)] if seq > 1 else []
    bit = 1
    while bit < dp:
        stages.append(("dp", bit))
        bit *= 2
    bit = 2
    while bit < seq:
        stages.append(("seq", bit))
        bit *= 2
    return stages


def sum_over(value, scale):
    stages = sum_stages()
    rows = value.shape[0]
    if stages is None or rows % (16 << len(stages)):
        return lax.psum(value, ("dp", "seq")) * scale
    sides = [(lax.axis_index(axis) // bit) % 2 for axis, bit in stages]
    for (axis, bit), side in zip(stages, sides):
        part = value.shape[0] // 2
        give = lax.dynamic_slice_in_dim(value, (1 - side) * part, part, 0).astype(BF16)
        keep = lax.dynamic_slice_in_dim(value, side * part, part, 0)
        value = keep + swapped(give, axis, bit).astype(F32)
    value = (value * scale).astype(BF16)
    for (axis, bit), side in reversed(list(zip(stages, sides))):
        other = swapped(value, axis, bit)
        low = jnp.where(side == 0, value, other)
        high = jnp.where(side == 0, other, value)
        value = jnp.concatenate([low, high], axis=0)
    return value.astype(F32)


def shards(events, gate_in, filters, proj, lengths, cotangent):
    users, block_len, chans = events.shape
    taps_len = filters.shape[0]
    reach = taps_len // block_len
    fwd_np, inv_np = tables(block_len)
    fwd, inv = jnp.asarray(fwd_np), jnp.asarray(inv_np)
    here = lax.axis_index("seq")
    first = here * block_len
    position = first + jnp.arange(block_len, dtype=jnp.int32)
    live = (position[None, :] < lengths[:, None]).astype(F32)[:, :, None]
    offsets = jnp.arange(reach + 1, dtype=jnp.int32) * block_len
    counts = lengths[None, :].astype(jnp.int32) - (first - offsets)[:, None]
    scal = jnp.concatenate(
        [(here % 2).astype(jnp.int32)[None], jnp.clip(counts, 0, block_len).reshape(-1)]
    )

    earlier, earlier_at = halo(events, reach, 1)
    spectra = filter_spectra(filters, fwd)

    n_tensor = lax.axis_size("tensor")
    cot_rows = cotangent.reshape(-1, chans)
    contract_last = (((1,), (1,)), ((), ()))
    contract_rows = (((0,), (0,)), ((), ()))
    if n_tensor == 2:
        mine = lax.axis_index("tensor")
        proj_own = lax.dynamic_slice_in_dim(proj, mine * chans, chans, 1)
        proj_other = lax.dynamic_slice_in_dim(proj, (1 - mine) * chans, chans, 1)
        cot_other = swapped(cot_rows, "tensor", 1)
        grad_acc = lax.dot_general(
            cot_rows, proj_own, contract_last, preferred_element_type=F32
        ) + lax.dot_general(cot_other, proj_other, contract_last, preferred_element_type=F32)
    else:
        cot_all = lax.all_gather(cot_rows, "tensor", axis=1, tiled=True)
        grad_acc = lax.dot_general(cot_all, proj, contract_last, preferred_element_type=F32)

    gate_f = gate_in.astype(F32)
    silu_g = gate_f * jax.nn.sigmoid(gate_f)
    grad_gated = grad_acc.reshape(users, block_len, chans) * live
    grad_conv = (grad_gated * silu_g).astype(BF16)
    later, later_at = halo(grad_conv, reach, -1)

    gated, grad_gate, filter_parts = conv_call(
        scal, earlier_at, earlier, grad_conv, gate_in, grad_gated, spectra, fwd, inv
    )
    rows = users * lax.axis_size("dp") * block_len * lax.axis_size("seq")
    scale = 1.0 / math.sqrt(rows)
    grad_filters = sum_over(filter_parts.reshape(taps_len, chans), scale)
    gated_rows = gated.reshape(-1, chans)
    if n_tensor == 2:
        part_other = jnp.dot(gated_rows, proj_other, preferred_element_type=F32)
        arrived = swapped(part_other.astype(BF16), "tensor", 1)
        out_rows = jnp.dot(gated_rows, proj_own, preferred_element_type=F32) + arrived.astype(F32)
        outer_own = lax.dot_general(gated_rows, cot_rows, contract_rows, preferred_element_type=F32)
        outer_other = lax.dot_general(
            gated_rows, cot_other, contract_rows, preferred_element_type=F32
        )
        sum_own, sum_other = sum_over(outer_own, scale), sum_over(outer_other, scale)
        grad_proj = jnp.concatenate(
            [
                jnp.where(mine == 0, sum_own, sum_other),
                jnp.where(mine == 0, sum_other, sum_own),
            ],
            axis=1,
        )
    else:
        partial_out = jnp.dot(gated_rows, proj, preferred_element_type=F32)
        out_rows = lax.psum_scatter(partial_out, "tensor", scatter_dimension=1, tiled=True)
        outer = lax.dot_general(gated_rows, cot_all, contract_rows, preferred_element_type=F32)
        grad_proj = sum_over(outer, scale)
    mixed = out_rows.astype(BF16).reshape(users, block_len, chans)
    grad_input = input_call(scal, later_at, later, spectra, fwd, inv)
    return (mixed, grad_input, grad_gate, grad_filters, grad_proj)


def solution(mesh):
    in_specs = (
        P("dp", "seq", "tensor"),
        P("dp", "seq", "tensor"),
        P(None, "tensor"),
        P("tensor", None),
        P("dp"),
        P("dp", "seq", "tensor"),
    )
    out_specs = (
        P("dp", "seq", "tensor"),
        P("dp", "seq", "tensor"),
        P("dp", "seq", "tensor"),
        P(None, "tensor"),
        P("tensor", None),
    )
    return jax.shard_map(shards, mesh=mesh, in_specs=in_specs, out_specs=out_specs, check_vma=False)
```
